1024 devices in a mesh: ctx: 64 (over z, x), head: 16 (over y, core).
Axes of the slice: x: 4, y: 8, z: 16, core: 2. Of those that a mesh axis runs over, the one named last changes fastest.
Arguments:
- query: bfloat16 [16384, 6144], P('ctx', 'head'), may hold values from -6 to 6
- key_in: bfloat16 [16384, 6144], P('ctx', 'head'), may hold values from -6 to 6
- value: bfloat16 [16384, 6144], P('ctx', 'head'), may hold values from -6 to 6
- out_weight: bfloat16 [6144, 6144], P('head'), may hold values from -0.078125 to 0.078125
- grad_layer: bfloat16 [16384, 6144], P(('ctx', 'head')), may hold values from -6 to 6
- decay_exp: int32 [48], P('head'), may hold values from 5 to 22
Outputs:
- grad_query: bfloat16 [16384, 6144], P('ctx', 'head')
- grad_key: bfloat16 [16384, 6144], P('ctx', 'head')
- grad_value: bfloat16 [16384, 6144], P('ctx', 'head')
The draws below stay inside these ranges and needn't reach their ends.
All inputs are finite; a program needn't handle non-finite values.
Results may differ from the reference program's by a relative error of at most 0.013.
Values may be sent and summed in bfloat16 or wider, within the bound.
A program may use at most 64 MiB of HBM per device.

```python
import jax
import jax.numpy as jnp
from jax import lax

HEADS = 48
DH = 128
MODEL = 6144
BLOCK = 256
TOKENS = 16384


def touch_ends(result, own_key, least, largest):
    dims = result.shape
    spot = [jax.random.randint(jax.random.fold_in(own_key, axis), (), 0, dims[axis]) for axis in range(len(dims))]
    result = result.at[tuple(spot)].set(least)
    longest = dims.index(max(dims))
    spot[longest] = (spot[longest] + 1) % dims[longest]
    return result.at[tuple(spot)].set(largest)


def block_levels(rng, extent, shards, smallest, top_value):
    def one(position, shards_of):
        draws = jax.random.uniform(jax.random.fold_in(jax.random.fold_in(rng, 6), position), (shards_of,), jnp.float32, smallest / len(shards), top_value / len(shards))
        return jnp.repeat(jnp.exp(draws), extent[position] // shards_of).reshape((-1,) + (1,) * (len(extent) - position - 1))

    level = one(*shards[0])
    for cut in shards[1:]:
        level = level * one(*cut)
    return level


def scatter_about(key, dims, deviation, most, cuts=(), dtype=jnp.bfloat16):
    result = deviation * jax.random.normal(key, dims, jnp.float32)
    if cuts:
        result = result * block_levels(key, dims, cuts, -0.22, 0.18)
    return jnp.clip(result, -most, most).astype(dtype)


def setup_inputs(seed: int = 0) -> dict:
    arg_keys = jax.random.split(jax.random.key(seed), 7)
    return {
        "query": scatter_about(arg_keys[0], (TOKENS, HEADS * DH), 1.0, 6.0, ((0, 64), (1, 16))),
        "key_in": scatter_about(arg_keys[1], (TOKENS, HEADS * DH), 1.0, 6.0, ((0, 64), (1, 16))),
        "value": scatter_about(arg_keys[2], (TOKENS, HEADS * DH), 1.0, 6.0, ((0, 64), (1, 16))),
        "out_weight": scatter_about(arg_keys[3], (HEADS * DH, MODEL), (HEADS * DH) ** -0.5, 0.078125, ((0, 16),)),
        "grad_layer": scatter_about(arg_keys[4], (TOKENS, MODEL), 1.0, 6.0, ((0, 1024),)),
        "decay_exp": touch_ends(jax.random.randint(arg_keys[5], (HEADS,), 5, 23), jax.random.fold_in(arg_keys[5], 1), 5, 22).astype(jnp.int32),
    }


EPSILON = 1e-06

def head_grads(packed):
    queries, keys_in, values_in, cotangent, log_rate = packed
    token_count = queries.shape[0]
    block_count = token_count // BLOCK
    highest = lax.Precision.HIGHEST
    offsets = jnp.arange(BLOCK).astype(jnp.float32)
    spread = offsets[:, None] - offsets[None, :]
    decay_mask = jnp.where(spread >= 0, jnp.exp(jnp.maximum(spread, 0.0) * log_rate), 0.0)
    query_decay = jnp.exp((offsets + 1.0) * log_rate)
    key_decay = jnp.exp((BLOCK - 1.0 - offsets) * log_rate)
    block_decay = jnp.exp(BLOCK * log_rate)

    def blocked(field):
        return field.reshape(block_count, BLOCK, DH)

    def forward_step(state, pieces):
        query_block, key_block, value_block = pieces
        scores = jnp.dot(query_block, key_block.T, preferred_element_type=jnp.float32)
        weights = (scores * decay_mask).astype(jnp.bfloat16)
        output = jnp.dot(weights, value_block, preferred_element_type=jnp.float32)
        output = output + jnp.dot(query_block.astype(jnp.float32) * query_decay[:, None], state, precision=highest)
        update = jnp.dot((key_block.astype(jnp.float32) * key_decay[:, None]).T, value_block.astype(jnp.float32), precision=highest)
        return (block_decay * state + update, (output, state))
    start = jnp.zeros((DH, DH), jnp.float32)
    _, (attended, states) = lax.scan(forward_step, start, (blocked(queries), blocked(keys_in), blocked(values_in)))
    square_mean = lax.optimization_barrier(jnp.mean(attended * attended, axis=-1, keepdims=True)) + EPSILON
    inverse = lax.rsqrt(square_mean)
    normed = attended * inverse
    cot_float = blocked(cotangent).astype(jnp.float32)
    dout = ((cot_float - normed * lax.optimization_barrier(jnp.mean(cot_float * normed, axis=-1, keepdims=True))) * inverse).astype(jnp.bfloat16)

    def backward_step(back, pieces):
        query_block, key_block, value_block, dout_block, state = pieces
        dout_float = dout_block.astype(jnp.float32)
        scores = jnp.dot(query_block, key_block.T, preferred_element_type=jnp.float32)
        weights = (scores * decay_mask).astype(jnp.bfloat16)
        dscores = jnp.dot(dout_block, value_block.T, preferred_element_type=jnp.float32)
        dweights = (dscores * decay_mask).astype(jnp.bfloat16)
        grad_q = jnp.dot(dweights, key_block, preferred_element_type=jnp.float32)
        grad_q = grad_q + jnp.dot(dout_float * query_decay[:, None], state.T, precision=highest)
        grad_k = jnp.dot(dweights.T, query_block, preferred_element_type=jnp.float32)
        grad_k = grad_k + jnp.dot(value_block.astype(jnp.float32) * key_decay[:, None], back.T, precision=highest)
        grad_v = jnp.dot(weights.T, dout_block, preferred_element_type=jnp.float32)
        grad_v = grad_v + jnp.dot(key_block.astype(jnp.float32) * key_decay[:, None], back, precision=highest)
        update = jnp.dot((query_block.astype(jnp.float32) * query_decay[:, None]).T, dout_float, precision=highest)
        return (block_decay * back + update, (grad_q.astype(jnp.bfloat16), grad_k.astype(jnp.bfloat16), grad_v.astype(jnp.bfloat16)))
    _, (grad_q, grad_k, grad_v) = lax.scan(backward_step, start, (blocked(queries), blocked(keys_in), blocked(values_in), dout, states), reverse=True)
    return (grad_q.reshape(token_count, DH), grad_k.reshape(token_count, DH), grad_v.reshape(token_count, DH))

def reference(query, key_in, value, out_weight, grad_layer, decay_exp):
    token_count = query.shape[0]
    log_rate = jnp.log1p(-jnp.exp2(-decay_exp.astype(jnp.float32)))
    dnormed = jnp.dot(grad_layer, out_weight.T, preferred_element_type=jnp.float32).astype(jnp.bfloat16)

    def heads_first(field):
        return jnp.transpose(field.reshape(token_count, HEADS, DH), (1, 0, 2))

    def rows_first(field):
        return jnp.transpose(field, (1, 0, 2)).reshape(token_count, HEADS * DH)
    grads = lax.map(head_grads, (heads_first(query), heads_first(key_in), heads_first(value), heads_first(dnormed), log_rate))
    return (rows_first(grads[0]), rows_first(grads[1]), rows_first(grads[2]))
```

```python
import functools

import jax
import jax.numpy as jnp
from jax import lax
from jax.experimental import pallas as pl
from jax.experimental.pallas import tpu as pltpu
from jax.sharding import PartitionSpec as P

MESH = pl.DeviceIdType.MESH
GROUP = 8
CHUNKS = 4
EPSILON = 1e-06
F32 = jnp.float32
BF16 = jnp.bfloat16
NN = (((1,), (0,)), ((), ()))
NT = (((1,), (1,)), ((), ()))
TN = (((0,), (0,)), ((), ()))


def dot(a, b, dims):
    return lax.dot_general(a, b, dims, preferred_element_type=F32)


def kernel(
    n_ctx,
    n_head,
    lr_ref,
    q_hbm,
    k_hbm,
    v_hbm,
    w_hbm,
    g_hbm,
    gq_ref,
    gk_ref,
    gv_ref,
    q,
    k,
    v,
    w,
    g,
    dn,
    scores,
    att,
    inv,
    dout,
    a_send,
    a_recv,
    pre,
    b_send,
    b_recv,
    carry,
    c_send,
    state,
    load_sem,
    ring_ssem,
    ring_rsem,
    pair_ssem,
    pair_rsem,
    a_ssem,
    a_rsem,
    b_ssem,
    b_rsem,
    c_ssem,
    c_rsem,
):
    rows, width = q.shape
    heads = width // 128
    shard_rows = rows // n_head
    chunk = g.shape[2] // CHUNKS
    piece = 128 // GROUP
    ny, n_hi = n_head // 2, n_ctx // GROUP
    half = ny // 2
    ctx, head = lax.axis_index("ctx"), lax.axis_index("head")
    y, core = head // 2, head % 2
    hi, lo = ctx // GROUP, ctx % GROUP

    loads = [
        pltpu.make_async_copy(src, dst, load_sem.at[i])
        for i, (src, dst) in enumerate(
            ((k_hbm, k), (v_hbm, v), (q_hbm, q), (g_hbm, g.at[head]), (w_hbm, w))
        )
    ]
    for load in loads:
        load.start()

    other = y * 2 + 1 - core
    partners = [(ctx, ((y + step) % ny) * 2 + core) for step in (1, ny - 1)] + [(ctx, other)]
    partners += [(hi * GROUP + (lo + step) % GROUP, head) for step in range(1, GROUP)]
    partners += [(((hi + step) % n_hi) * GROUP + lo, head) for step in range(1, n_hi)]
    barrier = pltpu.get_barrier_semaphore()
    for partner in partners:
        pl.semaphore_signal(barrier, inc=1, device_id=partner, device_id_type=MESH)
    pl.semaphore_wait(barrier, len(partners))

    def push(src, dst, ssem, rsem, device):
        return pltpu.make_async_remote_copy(
            src_ref=src,
            dst_ref=dst,
            send_sem=ssem,
            recv_sem=rsem,
            device_id=device,
            device_id_type=MESH,
        )

    def place(d, s, c):
        return ((y + (ny - s if d == 0 else s)) % ny) * 2 + c

    def carried(d, s, c):
        return s < half or (c < CHUNKS // 2) == (d == 0)

    def cols(c):
        return pl.ds(c * chunk, chunk)

    def ring(d, s, c):
        block = g.at[place(d, s, core), :, cols(c)]
        src = g_hbm.at[:, cols(c)] if s == 0 else block
        return push(
            src, block, ring_ssem.at[d, s, c], ring_rsem.at[d, s, c], (ctx, place(1 - d, 1, core))
        )

    def ring_in(d, s, c):
        block = g.at[place(d, s, core), :, cols(c)]
        return push(
            block, block, ring_ssem.at[d, s - 1, c], ring_rsem.at[d, s - 1, c], (ctx, other)
        )

    def pair(d, s, c):
        block = g.at[place(d, s, core), :, cols(c)]
        src = g_hbm.at[:, cols(c)] if s == 0 else block
        return push(src, block, pair_ssem.at[d, s, c], pair_rsem.at[d, s, c], (ctx, other))

    def pair_in(d, s, c):
        block = g.at[place(d, s, 1 - core), :, cols(c)]
        return push(block, block, pair_ssem.at[d, s, c], pair_rsem.at[d, s, c], (ctx, other))

    sent = []

    def start(copy):
        copy.start()
        sent.append(copy)

    for c in range(CHUNKS):
        for d in range(2):
            start(ring(d, 0, c))
    for c in range(CHUNKS):
        start(pair(0, 0, c))

    def ring_step(s):
        for c in range(CHUNKS):
            for d in range(2):
                if carried(d, s, c):
                    ring_in(d, s, c).wait_recv()
                    if s < half and carried(d, s + 1, c):
                        start(ring(d, s, c))
                    start(pair(d, s, c))

    def pair_step(s):
        for c in range(CHUNKS):
            for d in range(2):
                if carried(d, s, c) and (s > 0 or d == 0):
                    pair_in(d, s, c).wait_recv()

    def project(steps):
        blocks = []
        for s in steps:
            for d in range(2):
                if (s > 0 or d == 0) and (s < half or d == 0):
                    blocks += [place(d, s, core), place(d, s, 1 - core)]
        a = jnp.concatenate([g[block] for block in blocks], axis=0)
        out = dot(a, w[...], NT).astype(BF16)
        for i, block in enumerate(blocks):
            at = pl.ds(pl.multiple_of(block * shard_rows, shard_rows), shard_rows)
            dn[at, :] = out[i * shard_rows : (i + 1) * shard_rows]

    rates = [lr_ref[h] for h in range(heads)]
    lanes = jnp.concatenate([jnp.full((1, 128), rate, F32) for rate in rates], axis=1)
    offset = lax.broadcasted_iota(jnp.int32, (rows, 128), 0).astype(F32)

    def query_decay(h):
        return jnp.exp((offset + 1.0) * rates[h])

    def key_decay(h):
        return jnp.exp((rows - 1.0 - offset) * rates[h])

    def decay_mask(h):
        spread = lax.broadcasted_iota(jnp.int32, (rows, rows), 0) - lax.broadcasted_iota(
            jnp.int32, (rows, rows), 1
        )
        powers = jnp.exp(jnp.maximum(spread, 0).astype(F32) * rates[h])
        return jnp.where(spread >= 0, powers, 0.0)

    def device_decay(power):
        return jnp.exp((power * rows * 1.0) * lanes)

    def of(h):
        return slice(h * 128, (h + 1) * 128)

    def strip(place_of):
        return pl.ds(pl.multiple_of(place_of * piece, piece), piece)

    def peer(step):
        return (lo + step) % GROUP

    def a_start(t):
        for s in range(1, GROUP):
            start(
                push(
                    a_send.at[t, strip(peer(s))],
                    a_recv.at[t, lo],
                    a_ssem.at[t, s - 1],
                    a_rsem.at[t, s - 1],
                    (hi * GROUP + peer(s), head),
                )
            )
        a_recv[t, lo] = a_send[t, strip(lo)]

    def b_copy(t, s, target):
        return push(
            b_send.at[t],
            b_recv.at[t, s - 1],
            b_ssem.at[t, s - 1],
            b_rsem.at[t, s - 1],
            (target * GROUP + lo, head),
        )

    def a_finish(t):
        for s in range(1, GROUP):
            block = a_recv.at[t, peer(GROUP - s)]
            push(block, block, a_ssem.at[t, s - 1], a_rsem.at[t, s - 1], (ctx, other)).wait_recv()
        step = device_decay(1)
        total = jnp.zeros((piece, width), F32)
        for i in range(GROUP) if t == 0 else reversed(range(GROUP)):
            pre[t, i] = total
            total = step * total + a_recv[t, i].astype(F32)
        b_send[t] = total.astype(BF16)
        for s in range(1, n_hi):
            target = hi + s if t == 0 else hi - s

            @pl.when((target < n_hi) & (target >= 0))
            def _():
                b_copy(t, s, target).start()

    def b_finish(t):
        carry[...] = jnp.zeros_like(carry)
        for s in range(1, n_hi):
            source = hi - s if t == 0 else hi + s

            @pl.when((source < n_hi) & (source >= 0))
            def _():
                b_copy(t, s, hi).wait_recv()
                carry[...] += device_decay((s - 1) * GROUP) * b_recv[t, s - 1].astype(F32)

        for i in range(GROUP):
            power = i if t == 0 else GROUP - 1 - i
            c_send[t, i] = (pre[t, i] + device_decay(power) * carry[...]).astype(BF16)
        for s in range(1, GROUP):
            start(
                push(
                    c_send.at[t, peer(s)],
                    state.at[t, strip(lo)],
                    c_ssem.at[t, s - 1],
                    c_rsem.at[t, s - 1],
                    (hi * GROUP + peer(s), head),
                )
            )
        state[t, strip(lo), :] = c_send[t, lo]

    def b_drain(t):
        for s in range(1, n_hi):
            target = hi + s if t == 0 else hi - s

            @pl.when((target < n_hi) & (target >= 0))
            def _():
                b_copy(t, s, target).wait_send()

    def c_finish(t):
        for s in range(1, GROUP):
            block = state.at[t, strip(peer(GROUP - s))]
            push(block, block, c_ssem.at[t, s - 1], c_rsem.at[t, s - 1], (ctx, other)).wait_recv()

    loads[0].wait()
    loads[1].wait()
    for h in range(heads):
        decayed = (k[:, of(h)].astype(F32) * key_decay(h)).astype(BF16)
        a_send[0, :, of(h)] = dot(decayed, v[:, of(h)], TN).astype(BF16)
    a_start(0)
    loads[2].wait()
    ring_step(1)
    a_finish(0)
    for h in range(heads):
        product = dot(q[:, of(h)], k[:, of(h)], NT)
        weights = (product * decay_mask(h)).astype(BF16)
        scores[h] = weights
        att[:, of(h)] = dot(weights, v[:, of(h)], NN)
    for s in range(2, half):
        ring_step(s)
        if s == 2:
            b_finish(0)
    if half <= 2:
        b_finish(0)
    loads[3].wait()
    loads[4].wait()
    early = range(0, half - 1)
    for s in early:
        pair_step(s)
    project(early)
    c_finish(0)
    for h in range(heads):
        attended = att[:, of(h)] + query_decay(h) * dot(q[:, of(h)], state[0, :, of(h)], NN)
        inverse = lax.rsqrt(jnp.mean(attended * attended, axis=-1, keepdims=True) + EPSILON)
        att[:, of(h)] = attended * inverse
        inv[:, of(h)] = jnp.broadcast_to(inverse, (rows, 128))
    ring_step(half)
    pair_step(half - 1)
    pair_step(half)
    project(range(half - 1, half + 1))

    for h in range(heads):
        cot, normed = dn[:, of(h)].astype(F32), att[:, of(h)]
        along = jnp.mean(cot * normed, axis=-1, keepdims=True)
        grad = ((cot - normed * along) * inv[:, of(h)]).astype(BF16)
        dout[:, of(h)] = grad
        decayed = (q[:, of(h)].astype(F32) * query_decay(h)).astype(BF16)
        a_send[1, :, of(h)] = dot(decayed, grad, TN).astype(BF16)
    a_start(1)
    for h in range(heads):
        product = dot(dout[:, of(h)], v[:, of(h)], NT)
        dweights = (product * decay_mask(h)).astype(BF16)
        grad_q = dot(dweights, k[:, of(h)], NN)
        grad_q += query_decay(h) * dot(dout[:, of(h)], state[0, :, of(h)], NT)
        gq_ref[:, of(h)] = grad_q.astype(BF16)
        att[:, of(h)] = dot(dweights, q[:, of(h)], TN)
    a_finish(1)
    for h in range(heads):
        inv[:, of(h)] = dot(scores[h], dout[:, of(h)], TN)
    b_finish(1)
    c_finish(1)
    for h in range(heads):
        back = state[1, :, of(h)]
        decay = key_decay(h)
        gk_ref[:, of(h)] = (att[:, of(h)] + decay * dot(v[:, of(h)], back, NT)).astype(BF16)
        gv_ref[:, of(h)] = (inv[:, of(h)] + decay * dot(k[:, of(h)], back, NN)).astype(BF16)
    for copy in sent:
        copy.wait_send()
    b_drain(0)
    b_drain(1)


def body(n_ctx, n_head, query, key_in, value, out_weight, grad_layer, decay_exp):
    log_rate = jnp.log1p(-jnp.exp2(-decay_exp.astype(F32)))
    rows, width = query.shape
    model = grad_layer.shape[1]
    heads = decay_exp.shape[0]
    shard_rows = grad_layer.shape[0]
    half = n_head // 4
    piece = 128 // GROUP
    n_hi = n_ctx // GROUP
    vmem = pl.BlockSpec(memory_space=pltpu.VMEM)
    hbm = pl.BlockSpec(memory_space=pl.ANY)
    dma = pltpu.SemaphoreType.DMA
    out = jax.ShapeDtypeStruct((rows, width), BF16)
    return pl.pallas_call(
        functools.partial(kernel, n_ctx, n_head),
        out_shape=(out, out, out),
        in_specs=[pl.BlockSpec(memory_space=pltpu.SMEM)] + [hbm] * 5,
        out_specs=(vmem, vmem, vmem),
        scratch_shapes=[
            pltpu.VMEM((rows, width), BF16),
            pltpu.VMEM((rows, width), BF16),
            pltpu.VMEM((rows, width), BF16),
            pltpu.VMEM((width, model), BF16),
            pltpu.VMEM((n_head, shard_rows, model), BF16),
            pltpu.VMEM((rows, width), BF16),
            pltpu.VMEM((heads, rows, rows), BF16),
            pltpu.VMEM((rows, width), F32),
            pltpu.VMEM((rows, width), F32),
            pltpu.VMEM((rows, width), BF16),
            pltpu.VMEM((2, 128, width), BF16),
            pltpu.VMEM((2, GROUP, piece, width), BF16),
            pltpu.VMEM((2, GROUP, piece, width), F32),
            pltpu.VMEM((2, piece, width), BF16),
            pltpu.VMEM((2, max(n_hi - 1, 1), piece, width), BF16),
            pltpu.VMEM((piece, width), F32),
            pltpu.VMEM((2, GROUP, piece, width), BF16),
            pltpu.VMEM((2, 128, width), BF16),
            dma((5,)),
            dma((2, half, CHUNKS)),
            dma((2, half, CHUNKS)),
            dma((2, half + 1, CHUNKS)),
            dma((2, half + 1, CHUNKS)),
            dma((2, GROUP - 1)),
            dma((2, GROUP - 1)),
            dma((2, max(n_hi - 1, 1))),
            dma((2, max(n_hi - 1, 1))),
            dma((2, GROUP - 1)),
            dma((2, GROUP - 1)),
        ],
        compiler_params=pltpu.CompilerParams(collective_id=0, has_side_effects=True),
    )(log_rate, query, key_in, value, out_weight, grad_layer)


def solution(mesh):
    return jax.shard_map(
        functools.partial(body, mesh.shape["ctx"], mesh.shape["head"]),
        mesh=mesh,
        in_specs=(
            P("ctx", "head"),
            P("ctx", "head"),
            P("ctx", "head"),
            P("head", None),
            P(("ctx", "head"), None),
            P("head"),
        ),
        out_specs=(P("ctx", "head"), P("ctx", "head"), P("ctx", "head")),
        check_vma=False,
    )
```

```python
import functools

import jax
import jax.numpy as jnp
from jax import lax
from jax.experimental import pallas as pl
from jax.experimental.pallas import tpu as pltpu
from jax.sharding import PartitionSpec as P

MESH = pl.DeviceIdType.MESH
GROUP = 8
CHUNKS = 4
EPSILON = 1e-06
F32 = jnp.float32
BF16 = jnp.bfloat16
NN = (((1,), (0,)), ((), ()))
NT = (((1,), (1,)), ((), ()))
TN = (((0,), (0,)), ((), ()))


def dot(a, b, dims):
    return lax.dot_general(a, b, dims, preferred_element_type=F32)


def kernel(
    n_ctx,
    n_head,
    decay_ref,
    q_hbm,
    k_hbm,
    v_hbm,
    w_hbm,
    g_hbm,
    gq_ref,
    gk_ref,
    gv_ref,
    q,
    k,
    v,
    w,
    g,
    dn,
    scores,
    att,
    inv,
    dout,
    a_send,
    a_recv,
    pre,
    b_send,
    b_recv,
    carry,
    part,
    c_send,
    state,
    load_sem,
    ring_ssem,
    ring_rsem,
    pair_ssem,
    pair_rsem,
    a_ssem,
    a_rsem,
    b_ssem,
    b_rsem,
    c_ssem,
    c_rsem,
    ready,
):
    rows, width = q.shape
    heads = width // 128
    shard_rows = rows // n_head
    chunk = g.shape[2] // CHUNKS
    piece = 128 // GROUP
    ny, n_hi = n_head // 2, n_ctx // GROUP
    half = ny // 2
    ctx, head = lax.axis_index("ctx"), lax.axis_index("head")
    y, core = head // 2, head % 2
    hi, lo = ctx // GROUP, ctx % GROUP

    loads = [
        pltpu.make_async_copy(src, dst, load_sem.at[i])
        for i, (src, dst) in enumerate(
            ((k_hbm, k), (v_hbm, v), (q_hbm, q), (g_hbm, g.at[head]), (w_hbm, w))
        )
    ]
    for load in loads:
        load.start()

    other = y * 2 + 1 - core
    near = [(ctx, ((y + step) % ny) * 2 + core) for step in (1, ny - 1)] + [(ctx, other)]
    near += [(hi * GROUP + (lo + step) % GROUP, head) for step in range(1, GROUP)]
    barrier = pltpu.get_barrier_semaphore()
    for partner in near:
        pl.semaphore_signal(barrier, inc=1, device_id=partner, device_id_type=MESH)
    for s in range(1, n_hi):

        @pl.when(hi + s < n_hi)
        def _():
            later = ((hi + s) * GROUP + lo, head)
            pl.semaphore_signal(barrier, inc=1, device_id=later, device_id_type=MESH)

    pl.semaphore_wait(barrier, len(near) + hi)

    def greet():
        for s in range(1, n_hi):

            @pl.when(hi - s >= 0)
            def _():
                earlier = ((hi - s) * GROUP + lo, head)
                pl.semaphore_signal(
                    ready.at[s - 1], inc=1, device_id=earlier, device_id_type=MESH
                )

    def push(src, dst, ssem, rsem, device):
        return pltpu.make_async_remote_copy(
            src_ref=src,
            dst_ref=dst,
            send_sem=ssem,
            recv_sem=rsem,
            device_id=device,
            device_id_type=MESH,
        )

    def place(d, s, c):
        return ((y + (ny - s if d == 0 else s)) % ny) * 2 + c

    def carried(d, s, c):
        return s < half or (c < CHUNKS // 2) == (d == 0)

    def cols(c):
        return pl.ds(c * chunk, chunk)

    def ring(d, s, c):
        block = g.at[place(d, s, core), :, cols(c)]
        src = g_hbm.at[:, cols(c)] if s == 0 else block
        return push(
            src, block, ring_ssem.at[d, s, c], ring_rsem.at[d, s, c], (ctx, place(1 - d, 1, core))
        )

    def ring_in(d, s, c):
        block = g.at[place(d, s, core), :, cols(c)]
        return push(
            block, block, ring_ssem.at[d, s - 1, c], ring_rsem.at[d, s - 1, c], (ctx, other)
        )

    def pair(d, s, c):
        block = g.at[place(d, s, core), :, cols(c)]
        src = g_hbm.at[:, cols(c)] if s == 0 else block
        return push(src, block, pair_ssem.at[d, s, c], pair_rsem.at[d, s, c], (ctx, other))

    def pair_in(d, s, c):
        block = g.at[place(d, s, 1 - core), :, cols(c)]
        return push(block, block, pair_ssem.at[d, s, c], pair_rsem.at[d, s, c], (ctx, other))

    sent = []

    def start(copy):
        copy.start()
        sent.append(copy)

    for c in range(CHUNKS):
        for d in range(2):
            start(ring(d, 0, c))
    for c in range(CHUNKS):
        start(pair(0, 0, c))

    greet()

    def ring_chunk(s, c):
        for d in range(2):
            if carried(d, s, c):
                ring_in(d, s, c).wait_recv()
                if s < half and carried(d, s + 1, c):
                    start(ring(d, s, c))
                start(pair(d, s, c))

    def pair_chunk(s, c):
        for d in range(2):
            if carried(d, s, c) and (s > 0 or d == 0):
                pair_in(d, s, c).wait_recv()

    def blocks_of(steps):
        blocks = []
        for s in steps:
            for d in range(2):
                if (s > 0 or d == 0) and (s < half or d == 0):
                    blocks += [place(d, s, core), place(d, s, 1 - core)]
        return blocks

    def project(steps, c, first):
        blocks = blocks_of(steps)
        a = jnp.concatenate([g[block, :, cols(c)] for block in blocks], axis=0)
        out = dot(a, w[:, cols(c)], NT)
        at = slice(0, len(blocks) * shard_rows)
        part[at, :] = out if first else part[at, :] + out

    def place_rows(steps):
        for i, block in enumerate(blocks_of(steps)):
            at = pl.ds(pl.multiple_of(block * shard_rows, shard_rows), shard_rows)
            dn[at, :] = part[i * shard_rows : (i + 1) * shard_rows, :].astype(BF16)

    def rate_of(h):
        u = jnp.exp2(jnp.full((1, rows), -decay_ref[h].astype(F32)))
        tail = jnp.full_like(u, 1.0 / 9)
        for n in range(8, 0, -1):
            tail = 1.0 / n + u * tail
        return -u * tail

    rates = [rate_of(h) for h in range(heads)]
    lanes = jnp.concatenate([rate[:, :128] for rate in rates], axis=1)
    offset = lax.broadcasted_iota(jnp.int32, (rows, 128), 0).astype(F32)

    def query_decay(h):
        return jnp.exp((offset + 1.0) * rates[h][:, :128])

    def key_decay(h):
        return jnp.exp((rows - 1.0 - offset) * rates[h][:, :128])

    def decay_mask(h):
        spread = lax.broadcasted_iota(jnp.int32, (rows, rows), 0) - lax.broadcasted_iota(
            jnp.int32, (rows, rows), 1
        )
        powers = jnp.exp(jnp.maximum(spread, 0).astype(F32) * rates[h])
        return jnp.where(spread >= 0, powers, 0.0)

    def device_decay(power):
        return jnp.exp((power * rows * 1.0) * lanes)

    def of(h):
        return slice(h * 128, (h + 1) * 128)

    def strip(place_of):
        return pl.ds(pl.multiple_of(place_of * piece, piece), piece)

    def peer(step):
        return (lo + step) % GROUP

    def a_start(t):
        for s in range(1, GROUP):
            start(
                push(
                    a_send.at[t, strip(peer(s))],
                    a_recv.at[t, lo],
                    a_ssem.at[t, s - 1],
                    a_rsem.at[t, s - 1],
                    (hi * GROUP + peer(s), head),
                )
            )
        a_recv[t, lo] = a_send[t, strip(lo)]

    def b_copy(t, s, target):
        return push(
            b_send.at[t],
            b_recv.at[t, s - 1],
            b_ssem.at[t, s - 1],
            b_rsem.at[t, s - 1],
            (target * GROUP + lo, head),
        )

    def a_finish(t):
        for s in range(1, GROUP):
            block = a_recv.at[t, peer(GROUP - s)]
            push(block, block, a_ssem.at[t, s - 1], a_rsem.at[t, s - 1], (ctx, other)).wait_recv()
        step = device_decay(1)
        total = jnp.zeros((piece, width), F32)
        for i in range(GROUP) if t == 0 else reversed(range(GROUP)):
            pre[t, i] = total
            total = step * total + a_recv[t, i].astype(F32)
        b_send[t] = total.astype(BF16)

    def b_start(t, steps):
        for s in steps:
            target = hi + s if t == 0 else hi - s

            @pl.when((target < n_hi) & (target >= 0))
            def _():
                if t == 0:
                    pl.semaphore_wait(ready.at[s - 1], 1)
                b_copy(t, s, target).start()

    def b_finish(t):
        carry[...] = jnp.zeros_like(carry)
        for s in range(1, n_hi):
            source = hi - s if t == 0 else hi + s

            @pl.when((source < n_hi) & (source >= 0))
            def _():
                b_copy(t, s, hi).wait_recv()
                carry[...] += device_decay((s - 1) * GROUP) * b_recv[t, s - 1].astype(F32)

        for i in range(GROUP):
            power = i if t == 0 else GROUP - 1 - i
            c_send[t, i] = (pre[t, i] + device_decay(power) * carry[...]).astype(BF16)
        for s in range(1, GROUP):
            start(
                push(
                    c_send.at[t, peer(s)],
                    state.at[t, strip(lo)],
                    c_ssem.at[t, s - 1],
                    c_rsem.at[t, s - 1],
                    (hi * GROUP + peer(s), head),
                )
            )
        state[t, strip(lo), :] = c_send[t, lo]

    def b_drain(t):
        for s in range(1, n_hi):
            target = hi + s if t == 0 else hi - s

            @pl.when((target < n_hi) & (target >= 0))
            def _():
                b_copy(t, s, target).wait_send()

    def c_finish(t):
        for s in range(1, GROUP):
            block = state.at[t, strip(peer(GROUP - s))]
            push(block, block, c_ssem.at[t, s - 1], c_rsem.at[t, s - 1], (ctx, other)).wait_recv()

    loads[0].wait()
    loads[1].wait()
    for h in range(heads):
        decayed = (k[:, of(h)].astype(F32) * key_decay(h)).astype(BF16)
        a_send[0, :, of(h)] = dot(decayed, v[:, of(h)], TN).astype(BF16)
    a_start(0)
    loads[2].wait()
    for h in range(heads):
        product = dot(q[:, of(h)], k[:, of(h)], NT)
        weights = (product * decay_mask(h)).astype(BF16)
        scores[h] = weights
        att[:, of(h)] = dot(weights, v[:, of(h)], NN)
    loads[3].wait()
    loads[4].wait()
    early, late = range(0, half - 1), range(half - 1, half + 1)
    for s in range(1, half):
        for c in range(CHUNKS):
            ring_chunk(s, c)
            if (s, c) == (1, CHUNKS - 2):
                a_finish(0)
                b_start(0, range(1, min(3, n_hi)))
            if (s, c) == (2, 1) or (half == 2 and c == CHUNKS - 1):
                b_start(0, range(3, n_hi))
                b_finish(0)
            if s == half - 1:
                for earlier in early:
                    pair_chunk(earlier, c)
                project(early, c, c == 0)
    place_rows(early)
    c_finish(0)
    order = [c for pairs in zip(range(CHUNKS // 2), range(CHUNKS // 2, CHUNKS)) for c in pairs]
    for c in order:
        ring_chunk(half, c)
        if c == CHUNKS // 2:
            for h in range(heads):
                attended = att[:, of(h)] + query_decay(h) * dot(q[:, of(h)], state[0, :, of(h)], NN)
                inverse = lax.rsqrt(jnp.mean(attended * attended, axis=-1, keepdims=True) + EPSILON)
                att[:, of(h)] = attended * inverse
                inv[:, of(h)] = jnp.broadcast_to(inverse, (rows, 128))
    for c in order:
        for s in late:
            pair_chunk(s, c)
        project(late, c, c == 0)
    place_rows(late)

    for h in range(heads):
        cot, normed = dn[:, of(h)].astype(F32), att[:, of(h)]
        along = jnp.mean(cot * normed, axis=-1, keepdims=True)
        grad = ((cot - normed * along) * inv[:, of(h)]).astype(BF16)
        dout[:, of(h)] = grad
        decayed = (q[:, of(h)].astype(F32) * query_decay(h)).astype(BF16)
        a_send[1, :, of(h)] = dot(decayed, grad, TN).astype(BF16)
    a_start(1)
    for h in range(heads):
        product = dot(dout[:, of(h)], v[:, of(h)], NT)
        dweights = (product * decay_mask(h)).astype(BF16)
        grad_q = dot(dweights, k[:, of(h)], NN)
        grad_q += query_decay(h) * dot(dout[:, of(h)], state[0, :, of(h)], NT)
        gq_ref[:, of(h)] = grad_q.astype(BF16)
        att[:, of(h)] = dot(dweights, q[:, of(h)], TN)
    a_finish(1)
    b_start(1, range(1, n_hi))
    for h in range(heads):
        inv[:, of(h)] = dot(scores[h], dout[:, of(h)], TN)
    b_finish(1)
    c_finish(1)
    for h in range(heads):
        back = state[1, :, of(h)]
        decay = key_decay(h)
        gk_ref[:, of(h)] = (att[:, of(h)] + decay * dot(v[:, of(h)], back, NT)).astype(BF16)
        gv_ref[:, of(h)] = (inv[:, of(h)] + decay * dot(k[:, of(h)], back, NN)).astype(BF16)
    for copy in sent:
        copy.wait_send()
    b_drain(0)
    b_drain(1)


def store_kernel(gq_ref, gk_ref, gv_ref, gq_hbm, gk_hbm, gv_hbm, sem):
    copies = [
        pltpu.make_async_copy(src, dst, sem.at[i])
        for i, (src, dst) in enumerate(((gq_ref, gq_hbm), (gk_ref, gk_hbm), (gv_ref, gv_hbm)))
    ]
    for copy in copies:
        copy.start()
    for copy in copies:
        copy.wait()


def body(n_ctx, n_head, query, key_in, value, out_weight, grad_layer, decay_exp):
    rows, width = query.shape
    model = grad_layer.shape[1]
    heads = decay_exp.shape[0]
    shard_rows = grad_layer.shape[0]
    half = n_head // 4
    piece = 128 // GROUP
    n_hi = n_ctx // GROUP
    vmem = pl.BlockSpec(memory_space=pltpu.VMEM)
    hbm = pl.BlockSpec(memory_space=pltpu.HBM)
    dma = pltpu.SemaphoreType.DMA
    out = pltpu.VMEM((rows, width), BF16)
    grads = pl.pallas_call(
        functools.partial(kernel, n_ctx, n_head),
        out_shape=(out, out, out),
        in_specs=[pl.BlockSpec(memory_space=pltpu.SMEM)] + [hbm] * 5,
        out_specs=(vmem, vmem, vmem),
        scratch_shapes=[
            pltpu.VMEM((rows, width), BF16),
            pltpu.VMEM((rows, width), BF16),
            pltpu.VMEM((rows, width), BF16),
            pltpu.VMEM((width, model), BF16),
            pltpu.VMEM((n_head, shard_rows, model), BF16),
            pltpu.VMEM((rows, width), BF16),
            pltpu.VMEM((heads, rows, rows), BF16),
            pltpu.VMEM((rows, width), F32),
            pltpu.VMEM((rows, width), F32),
            pltpu.VMEM((rows, width), BF16),
            pltpu.VMEM((2, 128, width), BF16),
            pltpu.VMEM((2, GROUP, piece, width), BF16),
            pltpu.VMEM((2, GROUP, piece, width), F32),
            pltpu.VMEM((2, piece, width), BF16),
            pltpu.VMEM((2, max(n_hi - 1, 1), piece, width), BF16),
            pltpu.VMEM((piece, width), F32),
            pltpu.VMEM((rows, width), F32),
            pltpu.VMEM((2, GROUP, piece, width), BF16),
            pltpu.VMEM((2, 128, width), BF16),
            dma((5,)),
            dma((2, half, CHUNKS)),
            dma((2, half, CHUNKS)),
            dma((2, half + 1, CHUNKS)),
            dma((2, half + 1, CHUNKS)),
            dma((2, GROUP - 1)),
            dma((2, GROUP - 1)),
            dma((2, max(n_hi - 1, 1))),
            dma((2, max(n_hi - 1, 1))),
            dma((2, GROUP - 1)),
            dma((2, GROUP - 1)),
            pltpu.SemaphoreType.REGULAR((max(n_hi - 1, 1),)),
        ],
        compiler_params=pltpu.CompilerParams(
            collective_id=0, has_side_effects=True, vmem_limit_bytes=66 * 10**6
        ),
    )(decay_exp, query, key_in, value, out_weight, grad_layer)
    return pl.pallas_call(
        store_kernel,
        out_shape=(jax.ShapeDtypeStruct((rows, width), BF16),) * 3,
        in_specs=[vmem] * 3,
        out_specs=[hbm] * 3,
        scratch_shapes=[dma((3,))],
        compiler_params=pltpu.CompilerParams(vmem_limit_bytes=4 * 2**20),
    )(*grads)


def solution(mesh):
    return jax.shard_map(
        functools.partial(body, mesh.shape["ctx"], mesh.shape["head"]),
        mesh=mesh,
        in_specs=(
            P("ctx", "head"),
            P("ctx", "head"),
            P("ctx", "head"),
            P("head", None),
            P(("ctx", "head"), None),
            P("head"),
        ),
        out_specs=(P("ctx", "head"), P("ctx", "head"), P("ctx", "head")),
        check_vma=False,
    )
```
